32 devices in a mesh: dom: 8 (over y, x, core), st: 4 (over z).
Axes of the slice: x: 2, y: 2, z: 4, core: 2. Of those that a mesh axis runs over, the one named last changes fastest.
Arguments:
- start_block: bfloat16 [2, 64, 128, 729], P(None, 'dom', 'st'), may hold values from -48 to 48
- resident: bfloat16 [1024, 64, 729], P('st', 'dom'), may hold values from -0.09375 to 0.09375
- stiffness: bfloat16 [729, 729], replicated, may hold values from -0.21875 to 0.21875
- cell_scale: float32 [64], P('dom'), may hold values from 0.5 to 2
- potential: float32 [64, 729], P('dom'), may hold values from -1 to 1
- cell_count: int32 [8], P('dom'), may hold values from 2 to 8, as said below
- face_index: int32 [8, 2, 81], P('dom'), may hold values from 0 to 5831, as said below
Outputs:
- rotated: bfloat16 [2, 64, 128, 729], P(None, 'dom', 'st')
The draws below stay inside these ranges and needn't reach their ends.
Inputs may be any that keep to these rules, and one draw needn't show every extreme that they name: Domain d has cell_count[d] live cells in its first slots; some domain has 8 and some has 2. face_index[d, 0, :] lists each node of the last face of domain d's last live cell once, face_index[d, 1, :] each node of the first face of its cell 0 once, as flat indices cell * 729 + node; the k-th entries of face_index[d, 0] and face_index[d + 1, 1] are the same mesh node.
All inputs are finite; a program needn't handle non-finite values.
Results may differ from the reference program's by a relative error of at most 0.0075.
Values may be sent and summed in bfloat16 or wider, within the bound.
A program may use at most 64 MiB of HBM per device.

```python
import math
import jax
import jax.numpy as jnp
from jax import lax

NODES = 729
FACE = 81
STATES = 128
RES = 1024
BLOCKS = 2
CAP = 8
NCELL = 64


def domain_counts(key):
    base_key = jax.random.fold_in(key, 7)
    domain_total = NCELL // CAP
    counts = jax.random.randint(base_key, (domain_total,), 2, CAP + 1)
    chosen = jax.random.permutation(jax.random.fold_in(base_key, 1), domain_total)
    counts = counts.at[chosen[0]].set(CAP)
    counts = counts.at[chosen[1]].set(2)
    return counts.astype(jnp.int32)


def draw_cell_count(key, part):
    return domain_counts(key)


def face_order(sub_key):
    return jax.random.permutation(sub_key, FACE).astype(jnp.int32)


def draw_face_index(key, part):
    counts = domain_counts(key)
    domain_total = NCELL // CAP
    face_keys = jax.random.split(jax.random.fold_in(key, 11), domain_total)
    face_orders = jax.vmap(face_order)(face_keys)
    out_row = (counts[:, None] - 1) * NODES + (NODES - FACE) + face_orders
    previous = jnp.concatenate([face_orders[-1:], face_orders[:-1]], 0)
    return jnp.stack([out_row, previous], 1).astype(jnp.int32)


def draw_start_block(key, part):
    raw_key = jax.random.fold_in(key, 21)
    mix_key = jax.random.fold_in(key, 22)
    scale_key = jax.random.fold_in(key, 23)
    raw_values = jax.random.truncated_normal(raw_key, -4.0, 4.0, (BLOCKS, NCELL, STATES, NODES), jnp.float32)
    spread = jnp.exp(jax.random.uniform(scale_key, (NCELL,), jnp.float32, 0.0, math.log(10.0)))
    coupling = jax.random.truncated_normal(mix_key, -2.0, 2.0, (BLOCKS, STATES, STATES), jnp.float32)
    mixing = jnp.eye(STATES, dtype=jnp.float32)[None] + 0.25 / STATES ** 0.5 * coupling
    mixed_values = jnp.einsum('kcsn,kst->kctn', raw_values, mixing)
    mixed_values = mixed_values * spread[None, :, None, None]
    return jnp.clip(mixed_values, -48.0, 48.0).astype(jnp.bfloat16)


def steps_of(own_key, dims, pieces, low, top_value):
    factor_of = 1.0
    for dim, parts in pieces:
        heights = jax.random.uniform(jax.random.fold_in(jax.random.fold_in(own_key, 6), dim), (parts,), jnp.float32, low / len(pieces), top_value / len(pieces))
        factor_of = factor_of * jnp.repeat(jnp.exp(heights), dims[dim] // parts).reshape((-1,) + (1,) * (len(dims) - 1 - dim))
    return factor_of


def normal_values(key, shape, deviation, bound, cuts=(), kind=jnp.bfloat16):
    loudness = steps_of(key, shape, cuts, -0.22, 0.18) if cuts else 1.0
    drawn = jax.random.normal(key, shape, jnp.float32) * deviation * loudness
    return jnp.minimum(jnp.maximum(drawn, -bound), bound).astype(kind)


def setup_inputs(seed: int = 0) -> dict:
    splits = jax.random.split(jax.random.key(seed), 8)
    return {
        "start_block": draw_start_block(jax.random.fold_in(splits[7], 71), 0),
        "resident": normal_values(splits[1], (RES, NCELL, NODES), ((0.3 / (RES * NCELL * NODES) ** 0.5) ** 0.5), 0.09375, ((0, 4), (1, 8))),
        "stiffness": normal_values(splits[2], (NODES, NODES), NODES ** -0.5, 0.21875),
        "cell_scale": jnp.clip(jnp.exp(math.log(2.0) - 1.3862944 * jax.random.uniform(splits[3], (NCELL,), jnp.float32) ** steps_of(splits[3], (NCELL,), ((0, 8),), -0.2, 0.2)), 0.5, 2.0),
        "potential": jnp.clip(jax.random.uniform(splits[4], (NCELL, NODES), jnp.float32, -1.0, 1.0) * steps_of(splits[4], (NCELL, NODES), ((0, 8),), -0.4, 0.0), -1.0, 1.0),
        "cell_count": draw_cell_count(jax.random.fold_in(splits[7], 71), 0),
        "face_index": draw_face_index(jax.random.fold_in(splits[7], 71), 0),
    }


CENTER = 0.5
HALF_WIDTH = 2.0
EPSILON = 1e-06

def operate(in_field, stiffness, cell_scale, potential, live_slots, face_index):
    slot_count, state_count, node_count = in_field.shape
    local_sum = jnp.dot(in_field.reshape(slot_count * state_count, node_count), stiffness, preferred_element_type=jnp.float32).reshape(slot_count, state_count, node_count)
    local_sum = cell_scale[:, None, None] * local_sum + potential[:, None, :] * in_field.astype(jnp.float32)
    local_sum = local_sum.reshape(NCELL // CAP, CAP, state_count, node_count)
    right_face = local_sum[:, :-1, :, NODES - FACE:]
    left_face = local_sum[:, 1:, :, :FACE]
    pair_live = live_slots[:, 1:, None, None]
    local_sum = local_sum.at[:, :-1, :, NODES - FACE:].set(right_face + pair_live * left_face)
    local_sum = local_sum.at[:, 1:, :, :FACE].set(left_face + pair_live * right_face)
    domains = jnp.arange(NCELL // CAP).astype(jnp.int32)[:, None]
    out_cells = face_index[:, 0, :] // NODES
    out_nodes = face_index[:, 0, :] % NODES
    in_cells = face_index[:, 1, :] // NODES
    in_nodes = face_index[:, 1, :] % NODES
    outgoing = local_sum[domains, out_cells, :, out_nodes]
    incoming = local_sum[domains, in_cells, :, in_nodes]
    zero_face = jnp.zeros_like(outgoing[:1])
    from_left = jnp.concatenate([zero_face, outgoing[:-1]], 0)
    from_right = jnp.concatenate([incoming[1:], zero_face], 0)
    local_sum = local_sum.at[domains, in_cells, :, in_nodes].add(from_left)
    local_sum = local_sum.at[domains, out_cells, :, out_nodes].add(from_right)
    local_sum = local_sum * live_slots[:, :, None, None]
    return local_sum.reshape(slot_count, state_count, node_count)

def coefficients(correlation, inner_product_matrix, total_nodes):
    mean_square = jnp.diagonal(inner_product_matrix) / total_nodes + EPSILON
    inverse_root = lax.rsqrt(mean_square)
    normed = inner_product_matrix * inverse_root[:, None] * inverse_root[None, :] / total_nodes
    identity = jnp.eye(inner_product_matrix.shape[0], dtype=jnp.float32)
    mixing = inverse_root[:, None] * (1.5 * identity - 0.5 * normed)
    projected_states = jnp.dot(correlation, mixing, precision=lax.Precision.HIGHEST, preferred_element_type=jnp.float32)
    return (mixing.astype(jnp.bfloat16), projected_states.astype(jnp.bfloat16))

def reference(start_block, resident, stiffness, cell_scale, potential, cell_count, face_index):
    live_slots = (jnp.arange(CAP)[None, :] < cell_count[:, None]).astype(jnp.float32)
    live_mask = live_slots.reshape(-1).astype(jnp.bfloat16)[:, None, None]
    total_nodes = float(NCELL * NODES)

    def apply_h(in_field):
        return operate(in_field, stiffness, cell_scale, potential, live_slots, face_index)
    results = []
    for block_index in range(BLOCKS):
        first_states = start_block[block_index] * live_mask
        first_wide = first_states.astype(jnp.float32)
        step_one = ((apply_h(first_states) - CENTER * first_wide) / HALF_WIDTH).astype(jnp.bfloat16)
        filtered = (2.0 * (apply_h(step_one) - CENTER * step_one.astype(jnp.float32)) / HALF_WIDTH - first_wide).astype(jnp.bfloat16)
        filtered_broad_states = filtered.astype(jnp.float32)
        inner_product_matrix = jnp.einsum('ptw,phw->th', filtered_broad_states, filtered_broad_states)

        def add_correlation(domain, running_total):
            start_cell = (domain * CAP).astype(jnp.int32)
            resident_state_rows = lax.dynamic_slice_in_dim(resident, start_cell, CAP, 1).astype(jnp.float32)
            block_column_count = lax.dynamic_slice_in_dim(filtered_broad_states, start_cell, CAP, 0)
            return running_total + jnp.einsum('jpu,pzu->jz', resident_state_rows, block_column_count)
        correlation = lax.fori_loop(0, NCELL // CAP, add_correlation, jnp.zeros((RES, STATES), jnp.float32))
        mixing, projected_states = coefficients(correlation, inner_product_matrix, total_nodes)
        broad_mixing_weight = mixing.astype(jnp.float32)
        projected_broad_states = projected_states.astype(jnp.float32)

        def rotate(domain):
            start_cell = (domain * CAP).astype(jnp.int32)
            resident_state_rows = lax.dynamic_slice_in_dim(resident, start_cell, CAP, 1).astype(jnp.float32)
            block_column_count = lax.dynamic_slice_in_dim(filtered_broad_states, start_cell, CAP, 0)
            retained_portion = jnp.einsum('ghy,hw->gwy', block_column_count, broad_mixing_weight)
            series_term_sum = jnp.einsum('es,evd->vsd', projected_broad_states, resident_state_rows)
            return retained_portion - series_term_sum
        rotated = lax.map(rotate, jnp.arange(NCELL // CAP).astype(jnp.int32)).reshape(NCELL, STATES, NODES)
        results.append(rotated.astype(jnp.bfloat16) * live_mask)
    return jnp.stack(results)
```

```python
from functools import partial

import jax
import jax.numpy as jnp
from jax import lax
from jax.experimental import pallas as pl
from jax.experimental.pallas import tpu as pltpu
from jax.sharding import PartitionSpec as P

CENTER = 0.5
HALF_WIDTH = 2.0
EPSILON = 1e-06
F32 = jnp.float32
BF16 = jnp.bfloat16
RIGHT, LEFT = 0, 1


def dot_nn(a, b, precision=None):
    return lax.dot_general(
        a, b, (((1,), (0,)), ((), ())), precision=precision, preferred_element_type=F32
    )


def dot_nt(a, b, precision=None):
    return lax.dot_general(
        a, b, (((1,), (1,)), ((), ())), precision=precision, preferred_element_type=F32
    )


def kernel(
    sizes,
    flags_ref,
    start_ref,
    res_ref,
    stiff_ref,
    pot_ref,
    face_ref,
    out_ref,
    local,
    inner,
    states,
    part,
    part_recv,
    total,
    mix,
    proj,
    share,
    share_recv,
    face_out,
    face_in,
    face_send_sem,
    face_recv_sem,
    gather_send_sem,
    gather_recv_sem,
    one_send_sem,
    one_recv_sem,
    two_send_sem,
    two_recv_sem,
    share_send_sem,
    share_recv_sem,
):
    doms, sts, blocks, cells, width, nodes, face, res, rows = sizes
    total_states = sts * width
    total_nodes = float(doms * cells * nodes)
    window = (nodes - face) // 128 * 128
    offset = nodes - face - window
    d = lax.axis_index("dom")
    s = lax.axis_index("st")
    has_right, has_left = s < sts - 1, s > 0
    has_next, has_prev = d < doms - 1, d > 0
    own = pl.ds(pl.multiple_of(s * width, width), width)
    pending = []

    def dom_peer(k):
        return lax.rem(d + k, doms)

    barrier = pltpu.get_barrier_semaphore()

    def greet(k, carry):
        pl.semaphore_signal(
            barrier, inc=1, device_id={"dom": dom_peer(k)}, device_id_type=pl.DeviceIdType.MESH
        )
        return carry

    lax.fori_loop(1, doms, greet, 0)

    @pl.when(has_right)
    def _():
        pl.semaphore_signal(
            barrier, inc=1, device_id={"st": s + 1}, device_id_type=pl.DeviceIdType.MESH
        )

    @pl.when(has_left)
    def _():
        pl.semaphore_signal(
            barrier, inc=1, device_id={"st": s - 1}, device_id_type=pl.DeviceIdType.MESH
        )

    neighbours = has_right.astype(jnp.int32) + has_left.astype(jnp.int32)
    pl.semaphore_wait(barrier, doms - 1 + neighbours)

    def remote(src, dst, send_sem, recv_sem, axis, peer):
        return pltpu.make_async_remote_copy(
            src_ref=src,
            dst_ref=dst,
            send_sem=send_sem,
            recv_sem=recv_sem,
            device_id={axis: peer},
            device_id_type=pl.DeviceIdType.MESH,
        )

    def one_hot(row, first, count):
        node = lax.broadcasted_iota(jnp.int32, (count, face), 0) + first
        return jnp.where(face_ref[row : row + 1, :] == node, 1.0, 0.0).astype(F32)

    def rows_of(c):
        return slice(c * width, (c + 1) * width)

    def face_copy(step, b, way):
        return remote(
            face_out.at[step, b, way],
            face_in.at[step, b, way],
            face_send_sem.at[step, b, way],
            face_recv_sem.at[step, b, way],
            "dom",
            d + 1 if way == RIGHT else d - 1,
        )

    def apply_operator(step, b, field):
        local[...] = dot_nn(field(None), stiff_ref[...])
        last_tail = jnp.zeros((width, nodes - window), F32)
        for c in range(cells):
            value = flags_ref[0, c] * local[rows_of(c), :] + pot_ref[c : c + 1, :] * field(
                c
            ).astype(F32)
            local[rows_of(c), :] = value
            last_tail = last_tail + flags_ref[3, c] * value[:, window:]
        face_out[step, b, RIGHT] = dot_nn(
            last_tail, one_hot(0, window, nodes - window), lax.Precision.HIGHEST
        )
        face_out[step, b, LEFT] = dot_nn(
            local[rows_of(0), :face], one_hot(1, 0, face), lax.Precision.HIGHEST
        )
        for way, there in ((RIGHT, has_next), (LEFT, has_prev)):

            @pl.when(there)
            def _():
                face_copy(step, b, way).start()

            pending.append((there, partial(face_copy, step, b, way)))
        for c in range(cells - 1):
            pair = flags_ref[2, c + 1]
            tail = local[rows_of(c), window:]
            head = local[rows_of(c + 1), :face]
            padded = head
            if offset:
                padded = jnp.concatenate([jnp.zeros((width, offset), F32), head], axis=1)
            local[rows_of(c), window:] = tail + pair * padded
            local[rows_of(c + 1), :face] = head + pair * tail[:, offset:]
        for way, source in ((RIGHT, has_prev), (LEFT, has_next)):

            @pl.when(source)
            def _():
                face_copy(step, b, way).wait_recv()

            @pl.when(jnp.logical_not(source))
            def _():
                face_in[step, b, way] = jnp.zeros((width, face), F32)

        local[rows_of(0), :face] += dot_nt(
            face_in[step, b, RIGHT], one_hot(1, 0, face), lax.Precision.HIGHEST
        )
        tail_add = dot_nt(
            face_in[step, b, LEFT], one_hot(0, window, nodes - window), lax.Precision.HIGHEST
        )
        for c in range(cells):
            local[rows_of(c), window:] += flags_ref[3, c] * tail_add

    def filter_block(b):
        def first(c):
            if c is None:
                parts = [first(i) for i in range(cells)]
                return jnp.concatenate(parts, axis=0)
            return start_ref[b, c] * flags_ref[1, c].astype(BF16)

        def second(c):
            return inner[...] if c is None else inner[rows_of(c), :]

        apply_operator(0, b, first)
        for c in range(cells):
            value = flags_ref[1, c] * local[rows_of(c), :]
            inner[rows_of(c), :] = ((value - CENTER * first(c).astype(F32)) / HALF_WIDTH).astype(
                BF16
            )
        apply_operator(1, b, second)
        for c in range(cells):
            value = flags_ref[1, c] * local[rows_of(c), :]
            states[b, c, own, :] = (
                2.0 * (value - CENTER * second(c).astype(F32)) / HALF_WIDTH - first(c).astype(F32)
            ).astype(BF16)

    def gather_copy(b, way, shard):
        at = states.at[b, :, pl.ds(pl.multiple_of(shard * width, width), width), :]
        return remote(
            at,
            at,
            gather_send_sem.at[b, way, shard],
            gather_recv_sem.at[b, shard],
            "st",
            s + 1 if way == RIGHT else s - 1,
        )

    def gather_send(b, way, shard, there):
        @pl.when(there)
        def _():
            gather_copy(b, way, shard).start()

        pending.append((there, partial(gather_copy, b, way, shard)))

    def gather_start(b):
        gather_send(b, RIGHT, s, has_right)
        gather_send(b, LEFT, s, has_left)

    def gather_steps(b):
        for k in range(1, sts):
            for way, shard, here, more in (
                (RIGHT, s - k, s >= k, has_right),
                (LEFT, s + k, s + k < sts, has_left),
            ):

                @pl.when(here)
                def _():
                    gather_copy(b, way, shard).wait_recv()

                gather_send(b, way, shard, jnp.logical_and(here, more))

    def contract(b):
        part[b] = jnp.zeros(part.shape[1:], F32)

        def add_cell(c, carry):
            block = states[b, c]
            part[b, :res, :] += dot_nt(res_ref[c], block)
            part[b, res : res + total_states, :] += dot_nt(block, block)
            return carry

        lax.fori_loop(0, cells, add_cell, 0)

    def slice_of(peer):
        return pl.ds(pl.multiple_of(peer * rows, 8), rows)

    def one_copy(b, k):
        peer = dom_peer(k)
        return remote(
            part.at[b, slice_of(peer)],
            part_recv.at[b, k],
            one_send_sem.at[b, k],
            one_recv_sem.at[b, k],
            "dom",
            peer,
        )

    def two_copy(b, k):
        at = total.at[b, slice_of(d)]
        return remote(
            at, at, two_send_sem.at[b, k], two_recv_sem.at[b, k], "dom", dom_peer(k)
        )

    def from_peer(b, k):
        at = total.at[b, slice_of(dom_peer(doms - k))]
        return remote(
            at, at, two_send_sem.at[b, k], two_recv_sem.at[b, k], "dom", dom_peer(doms - k)
        )

    def all_reduce(b):
        def loop(body):
            def step(k, carry):
                body(k)
                return carry

            lax.fori_loop(1, doms, step, 0)

        loop(lambda k: one_copy(b, k).start())
        total[b, slice_of(d), :] = part[b, slice_of(d), :]

        def add(k):
            one_copy(b, k).wait_recv()
            total[b, slice_of(d), :] += part_recv[b, k]

        loop(add)
        loop(lambda k: two_copy(b, k).start())
        loop(lambda k: from_peer(b, k).wait_recv())

    def finish_reduce(b):
        def step(k, carry):
            one_copy(b, k).wait_send()
            two_copy(b, k).wait_send()
            return carry

        lax.fori_loop(1, doms, step, 0)

    def coefficients(b):
        gram = total[b, res : res + total_states, :]
        shape = (total_states, total_states)
        eye = (
            lax.broadcasted_iota(jnp.int32, shape, 0) == lax.broadcasted_iota(jnp.int32, shape, 1)
        ).astype(F32)
        along = jnp.sum(gram * eye, axis=0, keepdims=True) / total_nodes + EPSILON
        down = jnp.sum(gram * eye, axis=1, keepdims=True) / total_nodes + EPSILON
        root_i, root_j = lax.rsqrt(along), lax.rsqrt(down)
        mixing = root_i * (1.5 * eye - 0.5 * (gram * root_i * root_j / total_nodes))
        mix[b] = mixing.astype(BF16)
        proj[b] = dot_nt(mixing, total[b, :res, :], lax.Precision.HIGHEST).astype(BF16)

    def share_copy(b, t, way):
        return remote(
            share.at[b, t],
            share_recv.at[way, b, t],
            share_send_sem.at[b, t],
            share_recv_sem.at[way, b, t],
            "st",
            s + 1 if way == RIGHT else s - 1,
        )

    def targets():
        for j in range(sts - 1):
            far = sts - 1 - j
            yield far, RIGHT, far > s, has_left
            yield j, LEFT, j < s, has_right

    def share_start(b):
        for t, way, ahead, behind in targets():

            @pl.when(ahead)
            def _():
                def one(c, carry):
                    share[b, t, c] = dot_nn(
                        proj[b, t * width : (t + 1) * width, :], res_ref[c]
                    ).astype(BF16)
                    return carry

                lax.fori_loop(0, cells, one, 0)

            @pl.when(jnp.logical_and(ahead, jnp.logical_not(behind)))
            def _():
                share_copy(b, t, way).start()

            pending.append((ahead, partial(share_copy, b, t, way)))

    def share_forward(b):
        for t, way, ahead, behind in targets():

            @pl.when(jnp.logical_and(ahead, behind))
            def _():
                share_copy(b, t, way).wait_recv()

                def one(c, carry):
                    share[b, t, c] = (
                        share[b, t, c].astype(F32) + share_recv[way, b, t, c].astype(F32)
                    ).astype(BF16)
                    return carry

                lax.fori_loop(0, cells, one, 0)
                share_copy(b, t, way).start()

    def finish(b):
        def own_copy(way):
            return remote(
                share.at[b, s],
                share_recv.at[way, b, s],
                share_send_sem.at[b, s],
                share_recv_sem.at[way, b, s],
                "st",
                s + 1 if way == RIGHT else s - 1,
            )

        for c in range(cells):
            local[rows_of(c), :] = dot_nn(mix[b, own, :], states[b, c]) - dot_nn(
                proj[b, own, :], res_ref[c]
            )
        for way, source in ((RIGHT, has_left), (LEFT, has_right)):

            @pl.when(source)
            def _():
                own_copy(way).wait_recv()
                for c in range(cells):
                    local[rows_of(c), :] -= share_recv[way, b, s, c].astype(F32)

        for c in range(cells):
            out_ref[b, c] = local[rows_of(c), :].astype(BF16) * flags_ref[1, c].astype(BF16)

    filter_block(0)
    gather_start(0)
    for b in range(1, blocks):
        filter_block(b)
    for b in range(blocks):
        gather_steps(b)
        if b + 1 < blocks:
            gather_start(b + 1)
        contract(b)
        all_reduce(b)
        if b:
            share_forward(b - 1)
        coefficients(b)
        share_start(b)
        if b:
            finish(b - 1)
    share_forward(blocks - 1)
    finish(blocks - 1)
    for there, make in pending:

        @pl.when(there)
        def _():
            make().wait_send()

    for b in range(blocks):
        finish_reduce(b)


def on_device(start_block, resident, stiffness, cell_scale, potential, cell_count, face_index):
    blocks, cells, width, nodes = start_block.shape
    res = resident.shape[0]
    face = face_index.shape[2]
    doms, sts = lax.axis_size("dom"), lax.axis_size("st")
    total_states = sts * width
    rows = -(-(res + total_states) // (8 * doms)) * 8
    slot = jnp.arange(cells)
    live = (slot < cell_count[0]).astype(F32)
    last = (slot == cell_count[0] - 1).astype(F32)
    flags = jnp.stack([cell_scale, live, live, last])
    face_nodes = face_index[0] % nodes
    sizes = (doms, sts, blocks, cells, width, nodes, face, res, rows)
    dma = pltpu.SemaphoreType.DMA
    vmem = pl.BlockSpec(memory_space=pltpu.VMEM)
    return pl.pallas_call(
        partial(kernel, sizes),
        out_shape=jax.ShapeDtypeStruct((blocks, cells, width, nodes), BF16),
        in_specs=[pl.BlockSpec(memory_space=pltpu.SMEM)] + [vmem] * 5,
        out_specs=vmem,
        scratch_shapes=[
            pltpu.VMEM((cells * width, nodes), F32),
            pltpu.VMEM((cells * width, nodes), BF16),
            pltpu.VMEM((blocks, cells, total_states, nodes), BF16),
            pltpu.VMEM((blocks, doms * rows, total_states), F32),
            pltpu.VMEM((blocks, doms, rows, total_states), F32),
            pltpu.VMEM((blocks, doms * rows, total_states), F32),
            pltpu.VMEM((blocks, total_states, total_states), BF16),
            pltpu.VMEM((blocks, total_states, res), BF16),
            pltpu.VMEM((blocks, sts, cells, width, nodes), BF16),
            pltpu.VMEM((2, blocks, sts, cells, width, nodes), BF16),
            pltpu.VMEM((2, blocks, 2, width, face), F32),
            pltpu.VMEM((2, blocks, 2, width, face), F32),
            dma((2, blocks, 2)),
            dma((2, blocks, 2)),
            dma((blocks, 2, sts)),
            dma((blocks, sts)),
            dma((blocks, doms)),
            dma((blocks, doms)),
            dma((blocks, doms)),
            dma((blocks, doms)),
            dma((blocks, sts)),
            dma((2, blocks, sts)),
        ],
        compiler_params=pltpu.CompilerParams(
            collective_id=0, has_side_effects=True, vmem_limit_bytes=60 * 1024 * 1024
        ),
    )(
        flags,
        start_block,
        jnp.transpose(resident, (1, 0, 2)),
        stiffness,
        potential,
        face_nodes,
    )


def solution(mesh):
    return jax.shard_map(
        on_device,
        mesh=mesh,
        in_specs=(
            P(None, "dom", "st", None),
            P("st", "dom", None),
            P(),
            P("dom"),
            P("dom", None),
            P("dom"),
            P("dom", None, None),
        ),
        out_specs=P(None, "dom", "st", None),
        check_vma=False,
    )
```

```python
from functools import partial

import jax
import jax.numpy as jnp
from jax import lax
from jax.experimental import pallas as pl
from jax.experimental.pallas import tpu as pltpu
from jax.sharding import PartitionSpec as P

CENTER = 0.5
HALF_WIDTH = 2.0
EPSILON = 1e-06
F32 = jnp.float32
BF16 = jnp.bfloat16
RIGHT, LEFT = 0, 1


def dot_nn(a, b, precision=None):
    return lax.dot_general(
        a, b, (((1,), (0,)), ((), ())), precision=precision, preferred_element_type=F32
    )


def dot_nt(a, b, precision=None):
    return lax.dot_general(
        a, b, (((1,), (1,)), ((), ())), precision=precision, preferred_element_type=F32
    )


def kernel(
    sizes,
    scale_ref,
    count_ref,
    start_ref,
    res_hbm,
    stiff_ref,
    pot_ref,
    face_ref,
    out_ref,
    local,
    inner,
    states,
    part,
    part_recv,
    total,
    mix,
    proj,
    share,
    share_recv,
    res_in,
    res_wide,
    res_ref,
    res_near,
    proj_near,
    retained,
    face_out,
    face_in,
    face_send_sem,
    face_recv_sem,
    gather_send_sem,
    gather_recv_sem,
    one_send_sem,
    one_recv_sem,
    two_send_sem,
    two_recv_sem,
    share_send_sem,
    share_recv_sem,
    load_sem,
    near_send_sem,
    near_recv_sem,
    coef_send_sem,
    coef_recv_sem,
):
    doms, sts, blocks, cells, width, nodes, face, res, rows, moved = sizes
    total_states = sts * width
    total_nodes = float(doms * cells * nodes)
    window = (nodes - face) // 128 * 128
    offset = nodes - face - window
    d = lax.axis_index("dom")
    s = lax.axis_index("st")
    has_right, has_left = s < sts - 1, s > 0
    has_next, has_prev = d < doms - 1, d > 0
    own = pl.ds(pl.multiple_of(s * width, width), width)
    pending = []
    count = count_ref[0]
    scale = [scale_ref[c] for c in range(cells)]
    live = [jnp.where(c < count, 1.0, 0.0).astype(F32) for c in range(cells)]
    last = [jnp.where(c == count - 1, 1.0, 0.0).astype(F32) for c in range(cells)]
    load = pltpu.make_async_copy(res_hbm, res_in, load_sem)
    load.start()

    def dom_peer(k):
        return lax.rem(d + k, doms)

    barrier = pltpu.get_barrier_semaphore()

    def greet(k, carry):
        pl.semaphore_signal(
            barrier, inc=1, device_id={"dom": dom_peer(k)}, device_id_type=pl.DeviceIdType.MESH
        )
        return carry

    lax.fori_loop(1, doms, greet, 0)

    @pl.when(has_right)
    def _():
        pl.semaphore_signal(
            barrier, inc=1, device_id={"st": s + 1}, device_id_type=pl.DeviceIdType.MESH
        )

    @pl.when(has_left)
    def _():
        pl.semaphore_signal(
            barrier, inc=1, device_id={"st": s - 1}, device_id_type=pl.DeviceIdType.MESH
        )

    neighbours = has_right.astype(jnp.int32) + has_left.astype(jnp.int32)
    pl.semaphore_wait(barrier, doms - 1 + neighbours)

    def remote(src, dst, send_sem, recv_sem, axis, peer):
        return pltpu.make_async_remote_copy(
            src_ref=src,
            dst_ref=dst,
            send_sem=send_sem,
            recv_sem=recv_sem,
            device_id={axis: peer},
            device_id_type=pl.DeviceIdType.MESH,
        )

    def one_hot(row, first, extent):
        node = lax.broadcasted_iota(jnp.int32, (extent, face), 0) + first
        if row == 0:
            node = node + (count - 1) * nodes
        return jnp.where(face_ref[0, row : row + 1, :] == node, 1.0, 0.0).astype(F32)

    def mask(c):
        return live[c].astype(BF16)

    def relayout(chunk):
        at = slice(chunk * face, (chunk + 1) * face)
        wide = res_in[at].astype(F32).reshape(face * cells, res)
        for h in range(res // 128):
            lanes = slice(h * 128, (h + 1) * 128)
            res_wide[h] = wide[:, lanes]
            for c in range(cells):
                res_ref[c, at, lanes] = res_wide[h, pl.ds(c, face, stride=cells), :].astype(BF16)

    chunks = nodes // face

    def first_chunks():
        load.wait()
        for chunk in range(chunks // 2):
            relayout(chunk)

    def last_chunks():
        for chunk in range(chunks // 2, chunks):
            relayout(chunk)

    def rows_of(c):
        return slice(c * width, (c + 1) * width)

    def face_copy(step, b, way):
        return remote(
            face_out.at[step, b, way],
            face_in.at[step, b, way],
            face_send_sem.at[step, b, way],
            face_recv_sem.at[step, b, way],
            "dom",
            d + 1 if way == RIGHT else d - 1,
        )

    def apply_operator(step, b, field, meanwhile=None):
        local[...] = dot_nn(field(None), stiff_ref[...])
        last_tail = jnp.zeros((width, nodes - window), F32)
        for c in range(cells):
            value = scale[c] * local[rows_of(c), :] + pot_ref[c : c + 1, :] * field(
                c
            ).astype(F32)
            local[rows_of(c), :] = value
            last_tail = last_tail + last[c] * value[:, window:]
        face_out[step, b, RIGHT] = dot_nn(
            last_tail, one_hot(0, window, nodes - window), lax.Precision.HIGHEST
        )
        face_out[step, b, LEFT] = dot_nn(
            local[rows_of(0), :face], one_hot(1, 0, face), lax.Precision.HIGHEST
        )
        for way, there in ((RIGHT, has_next), (LEFT, has_prev)):

            @pl.when(there)
            def _():
                face_copy(step, b, way).start()

            pending.append((there, partial(face_copy, step, b, way)))
        for c in range(cells - 1):
            pair = live[c + 1]
            tail = local[rows_of(c), window:]
            head = local[rows_of(c + 1), :face]
            padded = head
            if offset:
                padded = jnp.concatenate([jnp.zeros((width, offset), F32), head], axis=1)
            local[rows_of(c), window:] = tail + pair * padded
            local[rows_of(c + 1), :face] = head + pair * tail[:, offset:]
        if meanwhile is not None:
            meanwhile()
        for way, source in ((RIGHT, has_prev), (LEFT, has_next)):

            @pl.when(source)
            def _():
                face_copy(step, b, way).wait_recv()

            @pl.when(jnp.logical_not(source))
            def _():
                face_in[step, b, way] = jnp.zeros((width, face), F32)

        local[rows_of(0), :face] += dot_nt(
            face_in[step, b, RIGHT], one_hot(1, 0, face), lax.Precision.HIGHEST
        )
        tail_add = dot_nt(
            face_in[step, b, LEFT], one_hot(0, window, nodes - window), lax.Precision.HIGHEST
        )
        for c in range(cells):
            local[rows_of(c), window:] += last[c] * tail_add

    def filter_block(b, one=None, two=None):
        def first(c):
            if c is None:
                parts = [first(i) for i in range(cells)]
                return jnp.concatenate(parts, axis=0)
            return start_ref[b, c] * mask(c)

        def second(c):
            return inner[...] if c is None else inner[rows_of(c), :]

        apply_operator(0, b, first, one)
        for c in range(cells):
            value = live[c] * local[rows_of(c), :]
            inner[rows_of(c), :] = ((value - CENTER * first(c).astype(F32)) / HALF_WIDTH).astype(
                BF16
            )
        apply_operator(1, b, second, two)
        for c in range(cells):
            value = live[c] * local[rows_of(c), :]
            states[b, c, own, :] = (
                2.0 * (value - CENTER * second(c).astype(F32)) / HALF_WIDTH - first(c).astype(F32)
            ).astype(BF16)

    def gather_copy(b, way, shard):
        at = states.at[b, :, pl.ds(pl.multiple_of(shard * width, width), width), :]
        return remote(
            at,
            at,
            gather_send_sem.at[b, way, shard],
            gather_recv_sem.at[b, shard],
            "st",
            s + 1 if way == RIGHT else s - 1,
        )

    def gather_send(b, way, shard, there):
        @pl.when(there)
        def _():
            gather_copy(b, way, shard).start()

        pending.append((there, partial(gather_copy, b, way, shard)))

    def gather_start(b):
        gather_send(b, RIGHT, s, has_right)
        gather_send(b, LEFT, s, has_left)

    def gather_steps(b):
        for k in range(1, sts):
            for way, shard, here, more in (
                (RIGHT, s - k, s >= k, has_right),
                (LEFT, s + k, s + k < sts, has_left),
            ):

                @pl.when(here)
                def _():
                    gather_copy(b, way, shard).wait_recv()

                gather_send(b, way, shard, jnp.logical_and(here, more))

    def contract(b):
        part[b] = jnp.zeros(part.shape[1:], F32)

        def add_cell(c, carry):
            block = states[b, c]
            found = dot_nn(block, res_ref[c])
            for h in range(res // total_states):
                at = slice(h * total_states, (h + 1) * total_states)
                part[b, at, :] += found[:, at]
            part[b, res : res + total_states, :] += dot_nt(block, block)
            return carry

        lax.fori_loop(0, cells, add_cell, 0)

    def slice_of(peer):
        return pl.ds(pl.multiple_of(peer * rows, 8), rows)

    def one_copy(b, k):
        peer = dom_peer(k)
        return remote(
            part.at[b, slice_of(peer)],
            part_recv.at[b, k],
            one_send_sem.at[b, k],
            one_recv_sem.at[b, k],
            "dom",
            peer,
        )

    def two_copy(b, k):
        at = total.at[b, slice_of(d)]
        return remote(
            at, at, two_send_sem.at[b, k], two_recv_sem.at[b, k], "dom", dom_peer(k)
        )

    def from_peer(b, k):
        at = total.at[b, slice_of(dom_peer(doms - k))]
        return remote(
            at, at, two_send_sem.at[b, k], two_recv_sem.at[b, k], "dom", dom_peer(doms - k)
        )

    def all_reduce(b):
        def loop(body):
            def step(k, carry):
                body(k)
                return carry

            lax.fori_loop(1, doms, step, 0)

        loop(lambda k: one_copy(b, k).start())
        total[b, slice_of(d), :] = part[b, slice_of(d), :]

        def add(k):
            one_copy(b, k).wait_recv()
            total[b, slice_of(d), :] += part_recv[b, k]

        loop(add)
        loop(lambda k: two_copy(b, k).start())
        loop(lambda k: from_peer(b, k).wait_recv())

    def finish_reduce(b):
        def step(k, carry):
            one_copy(b, k).wait_send()
            two_copy(b, k).wait_send()
            return carry

        lax.fori_loop(1, doms, step, 0)

    def coefficients(b):
        gram = total[b, res : res + total_states, :]
        shape = (total_states, total_states)
        eye = (
            lax.broadcasted_iota(jnp.int32, shape, 0) == lax.broadcasted_iota(jnp.int32, shape, 1)
        ).astype(F32)
        along = jnp.sum(gram * eye, axis=0, keepdims=True) / total_nodes + EPSILON
        down = jnp.sum(gram * eye, axis=1, keepdims=True) / total_nodes + EPSILON
        root_i, root_j = lax.rsqrt(along), lax.rsqrt(down)
        mixing = root_i * (1.5 * eye - 0.5 * (gram * root_i * root_j / total_nodes))
        mix[b] = mixing.astype(BF16)
        for h in range(res // total_states):
            at = slice(h * total_states, (h + 1) * total_states)
            proj[b, :, at] = dot_nn(mixing, total[b, at, :], lax.Precision.HIGHEST).astype(BF16)

    def to(way):
        return s + 1 if way == RIGHT else s - 1

    origin = {RIGHT: s == 0, LEFT: s == sts - 1}
    sends = {RIGHT: has_right, LEFT: has_left}
    receives = {RIGHT: has_left, LEFT: has_right}
    near_end = {RIGHT: s == 1, LEFT: s == sts - 2}
    pieces = ((0, moved), (moved, cells))
    both = jnp.logical_and

    def near_copy(way, c):
        return remote(
            res_ref.at[c],
            res_near.at[way, c],
            near_send_sem.at[way, c],
            near_recv_sem.at[way, c],
            "st",
            to(way),
        )

    def near_start(c):
        for way in (RIGHT, LEFT):
            there = both(origin[way], sends[way])

            @pl.when(there)
            def _():
                near_copy(way, c).start()

            pending.append((there, partial(near_copy, way, c)))

    def near_wait():
        for way in (RIGHT, LEFT):

            @pl.when(near_end[way])
            def _():
                for c in range(moved):
                    near_copy(way, c).wait_recv()

    def coef_copy(b, way):
        return remote(
            proj.at[b],
            proj_near.at[way, b],
            coef_send_sem.at[way, b],
            coef_recv_sem.at[way, b],
            "st",
            to(way),
        )

    def coef_start(b):
        for way in (RIGHT, LEFT):
            there = both(origin[way], sends[way])

            @pl.when(there)
            def _():
                coef_copy(b, way).start()

            pending.append((there, partial(coef_copy, b, way)))

    def share_copy(b, t, way, piece):
        at = pl.ds(pieces[piece][0], pieces[piece][1] - pieces[piece][0])
        return remote(
            share.at[b, t, at],
            share_recv.at[way, b, t, at],
            share_send_sem.at[b, t, piece],
            share_recv_sem.at[way, b, t, piece],
            "st",
            to(way),
        )

    def targets():
        for j in range(sts - 1):
            far = sts - 1 - j
            yield far, RIGHT, far > s
            yield j, LEFT, j < s

    def share_start(b):
        def one(c, carry):
            found = dot_nt(proj[b], res_ref[c])
            for t in range(sts):
                share[b, t, c] = found[t * width : (t + 1) * width, :].astype(BF16)
            return carry

        lax.fori_loop(0, cells, one, 0)
        for t, way, ahead in targets():

            @pl.when(both(ahead, origin[way]))
            def _():
                share_copy(b, t, way, 1).start()

            for piece in (0, 1):
                there = ahead if piece else both(ahead, jnp.logical_not(origin[way]))
                pending.append((there, partial(share_copy, b, t, way, piece)))

    def retain(b):
        def one(c, carry):
            retained[b, c] = dot_nn(mix[b, own, :], states[b, c]) - dot_nt(
                proj[b, own, :], res_ref[c]
            )
            return carry

        lax.fori_loop(0, cells, one, 0)

    def near_share(b):
        for way in (RIGHT, LEFT):

            @pl.when(near_end[way])
            def _():
                coef_copy(b, way).wait_recv()
                for c in range(moved):
                    found = dot_nt(proj_near[way, b], res_near[way, c])
                    for t in range(sts):
                        passed = t > s if way == RIGHT else t < s

                        @pl.when(passed)
                        def _():
                            share[b, t, c] = (
                                share[b, t, c].astype(F32)
                                + found[t * width : (t + 1) * width, :]
                            ).astype(BF16)

                        @pl.when(t == s)
                        def _():
                            retained[b, c] -= found[t * width : (t + 1) * width, :]

    def share_forward(b):
        for piece in (0, 1):
            for t, way, ahead in targets():

                @pl.when(both(ahead, jnp.logical_not(origin[way])))
                def _():
                    def absorb():
                        share_copy(b, t, way, piece).wait_recv()

                        def one(c, carry):
                            share[b, t, c] = (
                                share[b, t, c].astype(F32) + share_recv[way, b, t, c].astype(F32)
                            ).astype(BF16)
                            return carry

                        lax.fori_loop(*pieces[piece], one, 0)

                    if piece:
                        absorb()
                    else:
                        pl.when(jnp.logical_not(near_end[way]))(absorb)
                    share_copy(b, t, way, piece).start()

    def finish(b):
        for piece in (0, 1):
            for way in (RIGHT, LEFT):
                source = receives[way]
                if piece == 0:
                    source = both(source, jnp.logical_not(near_end[way]))

                @pl.when(source)
                def _():
                    share_copy(b, s, way, piece).wait_recv()

                    def one(c, carry):
                        retained[b, c] -= share_recv[way, b, s, c].astype(F32)
                        return carry

                    lax.fori_loop(*pieces[piece], one, 0)

            for c in range(*pieces[piece]):
                out_ref[b, c] = retained[b, c].astype(BF16) * mask(c)

    filter_block(0, first_chunks, last_chunks)
    gather_start(0)
    for c in range(moved):
        near_start(c)
    for b in range(1, blocks):
        filter_block(b)
    for b in range(blocks):
        gather_steps(b)
        if b + 1 < blocks:
            gather_start(b + 1)
        contract(b)
        all_reduce(b)
        if b:
            share_forward(b - 1)
        else:
            near_wait()
        coefficients(b)
        coef_start(b)
        share_start(b)
        retain(b)
        near_share(b)
        if b:
            finish(b - 1)
    share_forward(blocks - 1)
    finish(blocks - 1)
    for there, make in pending:

        @pl.when(there)
        def _():
            make().wait_send()

    for b in range(blocks):
        finish_reduce(b)


def on_device(start_block, resident, stiffness, cell_scale, potential, cell_count, face_index):
    blocks, cells, width, nodes = start_block.shape
    res = resident.shape[0]
    face = face_index.shape[2]
    doms, sts = lax.axis_size("dom"), lax.axis_size("st")
    total_states = sts * width
    rows = -(-(res + total_states) // (8 * doms)) * 8
    moved = cells // 4
    sizes = (doms, sts, blocks, cells, width, nodes, face, res, rows, moved)
    dma = pltpu.SemaphoreType.DMA
    vmem = pl.BlockSpec(memory_space=pltpu.VMEM)
    smem = pl.BlockSpec(memory_space=pltpu.SMEM)
    return pl.pallas_call(
        partial(kernel, sizes),
        out_shape=jax.ShapeDtypeStruct((blocks, cells, width, nodes), BF16),
        in_specs=[smem, smem, vmem, pl.BlockSpec(memory_space=pl.ANY), vmem, vmem, vmem],
        out_specs=vmem,
        scratch_shapes=[
            pltpu.VMEM((cells * width, nodes), F32),
            pltpu.VMEM((cells * width, nodes), BF16),
            pltpu.VMEM((blocks, cells, total_states, nodes), BF16),
            pltpu.VMEM((blocks, doms * rows, total_states), F32),
            pltpu.VMEM((blocks, doms, rows, total_states), F32),
            pltpu.VMEM((blocks, doms * rows, total_states), F32),
            pltpu.VMEM((blocks, total_states, total_states), BF16),
            pltpu.VMEM((blocks, total_states, res), BF16),
            pltpu.VMEM((blocks, sts, cells, width, nodes), BF16),
            pltpu.VMEM((2, blocks, sts, cells, width, nodes), BF16),
            pltpu.VMEM((nodes, cells, res), BF16),
            pltpu.VMEM((res // 128, face * cells, 128), F32),
            pltpu.VMEM((cells, nodes, res), BF16),
            pltpu.VMEM((2, moved, nodes, res), BF16),
            pltpu.VMEM((2, blocks, total_states, res), BF16),
            pltpu.VMEM((blocks, cells, width, nodes), F32),
            pltpu.VMEM((2, blocks, 2, width, face), F32),
            pltpu.VMEM((2, blocks, 2, width, face), F32),
            dma((2, blocks, 2)),
            dma((2, blocks, 2)),
            dma((blocks, 2, sts)),
            dma((blocks, sts)),
            dma((blocks, doms)),
            dma((blocks, doms)),
            dma((blocks, doms)),
            dma((blocks, doms)),
            dma((blocks, sts, 2)),
            dma((2, blocks, sts, 2)),
            dma,
            dma((2, moved)),
            dma((2, moved)),
            dma((2, blocks)),
            dma((2, blocks)),
        ],
        compiler_params=pltpu.CompilerParams(
            collective_id=0, has_side_effects=True, vmem_limit_bytes=60 * 1024 * 1024
        ),
    )(
        cell_scale,
        cell_count,
        start_block,
        jnp.transpose(resident, (2, 1, 0)),
        stiffness,
        potential,
        face_index,
    )


def solution(mesh):
    return jax.shard_map(
        on_device,
        mesh=mesh,
        in_specs=(
            P(None, "dom", "st", None),
            P("st", "dom", None),
            P(),
            P("dom"),
            P("dom", None),
            P("dom"),
            P("dom", None, None),
        ),
        out_specs=P(None, "dom", "st", None),
        check_vma=False,
    )
```

```python
from functools import partial

import jax
import jax.numpy as jnp
from jax import lax
from jax.experimental import pallas as pl
from jax.experimental.pallas import tpu as pltpu
from jax.sharding import PartitionSpec as P

CENTER = 0.5
HALF_WIDTH = 2.0
EPSILON = 1e-06
F32 = jnp.float32
BF16 = jnp.bfloat16
RIGHT, LEFT = 0, 1


def dot_nn(a, b, precision=None):
    return lax.dot_general(
        a, b, (((1,), (0,)), ((), ())), precision=precision, preferred_element_type=F32
    )


def dot_nt(a, b, precision=None):
    return lax.dot_general(
        a, b, (((1,), (1,)), ((), ())), precision=precision, preferred_element_type=F32
    )


def kernel(
    sizes,
    scale_ref,
    count_ref,
    start_ref,
    res_hbm,
    stiff_ref,
    pot_ref,
    face_ref,
    out_ref,
    local,
    inner,
    states,
    part,
    part_recv,
    total,
    mix,
    proj,
    share,
    share_recv,
    res_in,
    res_wide,
    res_ref,
    res_near,
    proj_near,
    retained,
    face_out,
    face_in,
    face_send_sem,
    face_recv_sem,
    gather_send_sem,
    gather_recv_sem,
    one_send_sem,
    one_recv_sem,
    two_send_sem,
    two_recv_sem,
    share_send_sem,
    share_recv_sem,
    load_sem,
    near_send_sem,
    near_recv_sem,
    coef_send_sem,
    coef_recv_sem,
):
    doms, sts, blocks, cells, width, nodes, face, res, rows, moved = sizes
    total_states = sts * width
    total_nodes = float(doms * cells * nodes)
    window = (nodes - face) // 128 * 128
    offset = nodes - face - window
    d = lax.axis_index("dom")
    s = lax.axis_index("st")
    has_right, has_left = s < sts - 1, s > 0
    has_next, has_prev = d < doms - 1, d > 0
    own = pl.ds(pl.multiple_of(s * width, width), width)
    pending = []
    both = jnp.logical_and
    count = count_ref[0]
    scale = [scale_ref[c] for c in range(cells)]
    live = [jnp.where(c < count, 1.0, 0.0).astype(F32) for c in range(cells)]
    last = [jnp.where(c == count - 1, 1.0, 0.0).astype(F32) for c in range(cells)]
    load = pltpu.make_async_copy(res_hbm, res_in, load_sem)
    load.start()

    def dom_peer(k):
        return lax.rem(d + k, doms)

    barrier = pltpu.get_barrier_semaphore()

    def greet(k, carry):
        pl.semaphore_signal(
            barrier, inc=1, device_id={"dom": dom_peer(k)}, device_id_type=pl.DeviceIdType.MESH
        )
        return carry

    lax.fori_loop(1, doms, greet, 0)

    @pl.when(has_right)
    def _():
        pl.semaphore_signal(
            barrier, inc=1, device_id={"st": s + 1}, device_id_type=pl.DeviceIdType.MESH
        )

    @pl.when(has_left)
    def _():
        pl.semaphore_signal(
            barrier, inc=1, device_id={"st": s - 1}, device_id_type=pl.DeviceIdType.MESH
        )

    neighbours = has_right.astype(jnp.int32) + has_left.astype(jnp.int32)
    pl.semaphore_wait(barrier, doms - 1 + neighbours)

    def remote(src, dst, send_sem, recv_sem, axis, peer):
        return pltpu.make_async_remote_copy(
            src_ref=src,
            dst_ref=dst,
            send_sem=send_sem,
            recv_sem=recv_sem,
            device_id={axis: peer},
            device_id_type=pl.DeviceIdType.MESH,
        )

    def one_hot(row, first, extent):
        node = lax.broadcasted_iota(jnp.int32, (extent, face), 0) + first
        if row == 0:
            node = node + (count - 1) * nodes
        return jnp.where(face_ref[0, row : row + 1, :] == node, 1.0, 0.0).astype(F32)

    def mask(c):
        return live[c].astype(BF16)

    def relayout(chunk):
        at = slice(chunk * face, (chunk + 1) * face)
        wide = res_in[at].astype(F32).reshape(face * cells, res)
        for h in range(res // 128):
            lanes = slice(h * 128, (h + 1) * 128)
            res_wide[h] = wide[:, lanes]
            for c in range(cells):
                res_ref[c, at, lanes] = res_wide[h, pl.ds(c, face, stride=cells), :].astype(BF16)

    chunks = nodes // face

    def first_chunks():
        load.wait()
        for chunk in range(chunks // 2):
            relayout(chunk)

    def last_chunks():
        for chunk in range(chunks // 2, chunks):
            relayout(chunk)

    def rows_of(c):
        return slice(c * width, (c + 1) * width)

    def face_copy(step, b, way):
        return remote(
            face_out.at[step, b, way],
            face_in.at[step, b, way],
            face_send_sem.at[step, b, way],
            face_recv_sem.at[step, b, way],
            "dom",
            d + 1 if way == RIGHT else d - 1,
        )

    def apply_operator(step, b, field, meanwhile=None):
        local[...] = dot_nn(field(None), stiff_ref[...])
        last_tail = jnp.zeros((width, nodes - window), F32)
        for c in range(cells):
            value = scale[c] * local[rows_of(c), :] + pot_ref[c : c + 1, :] * field(
                c
            ).astype(F32)
            local[rows_of(c), :] = value
            last_tail = last_tail + last[c] * value[:, window:]
        face_out[step, b, RIGHT] = dot_nn(
            last_tail, one_hot(0, window, nodes - window), lax.Precision.HIGHEST
        )
        face_out[step, b, LEFT] = dot_nn(
            local[rows_of(0), :face], one_hot(1, 0, face), lax.Precision.HIGHEST
        )
        for way, there in ((RIGHT, has_next), (LEFT, has_prev)):

            @pl.when(there)
            def _():
                face_copy(step, b, way).start()

            pending.append((there, partial(face_copy, step, b, way)))
        for c in range(cells - 1):
            pair = live[c + 1]
            tail = local[rows_of(c), window:]
            head = local[rows_of(c + 1), :face]
            padded = head
            if offset:
                padded = jnp.concatenate([jnp.zeros((width, offset), F32), head], axis=1)
            local[rows_of(c), window:] = tail + pair * padded
            local[rows_of(c + 1), :face] = head + pair * tail[:, offset:]
        if meanwhile is not None:
            meanwhile()
        for way, source in ((RIGHT, has_prev), (LEFT, has_next)):

            @pl.when(source)
            def _():
                face_copy(step, b, way).wait_recv()

            @pl.when(jnp.logical_not(source))
            def _():
                face_in[step, b, way] = jnp.zeros((width, face), F32)

        local[rows_of(0), :face] += dot_nt(
            face_in[step, b, RIGHT], one_hot(1, 0, face), lax.Precision.HIGHEST
        )
        tail_add = dot_nt(
            face_in[step, b, LEFT], one_hot(0, window, nodes - window), lax.Precision.HIGHEST
        )
        for c in range(cells):
            local[rows_of(c), window:] += last[c] * tail_add

    def filter_block(b, one=None, two=None):
        def first(c):
            if c is None:
                parts = [first(i) for i in range(cells)]
                return jnp.concatenate(parts, axis=0)
            return start_ref[b, c] * mask(c)

        def second(c):
            return inner[...] if c is None else inner[rows_of(c), :]

        apply_operator(0, b, first, one)
        for c in range(cells):
            value = live[c] * local[rows_of(c), :]
            inner[rows_of(c), :] = ((value - CENTER * first(c).astype(F32)) / HALF_WIDTH).astype(
                BF16
            )
        apply_operator(1, b, second, two)
        for c in range(cells):
            value = live[c] * local[rows_of(c), :]
            states[b, c, own, :] = (
                2.0 * (value - CENTER * second(c).astype(F32)) / HALF_WIDTH - first(c).astype(F32)
            ).astype(BF16)

    def gather_copy(b, way, shard):
        at = states.at[b, :, pl.ds(pl.multiple_of(shard * width, width), width), :]
        return remote(
            at,
            at,
            gather_send_sem.at[b, way, shard],
            gather_recv_sem.at[b, shard],
            "st",
            s + 1 if way == RIGHT else s - 1,
        )

    def gather_send(b, way, shard, there):
        @pl.when(there)
        def _():
            gather_copy(b, way, shard).start()

        pending.append((there, partial(gather_copy, b, way, shard)))

    def gather_start(b, k):
        gather_send(b, RIGHT, s, both(has_right, s == k))
        gather_send(b, LEFT, s, both(has_left, s + k == sts - 1))

    def gather_steps(b):
        for k in range(1, sts):
            for way, shard, here, more in (
                (RIGHT, s - k, s >= k, has_right),
                (LEFT, s + k, s + k < sts, has_left),
            ):

                @pl.when(here)
                def _():
                    gather_copy(b, way, shard).wait_recv()

                gather_send(b, way, shard, both(here, more))
            if b + 1 < blocks:
                gather_start(b + 1, k)

    def contract(b):
        part[b] = jnp.zeros(part.shape[1:], F32)

        def add_cell(c, carry):
            block = states[b, c]
            found = dot_nn(block, res_ref[c])
            for h in range(res // total_states):
                at = slice(h * total_states, (h + 1) * total_states)
                part[b, at, :] += found[:, at]
            part[b, res : res + total_states, :] += dot_nt(block, block)
            return carry

        lax.fori_loop(0, cells, add_cell, 0)

    def slice_of(peer):
        return pl.ds(pl.multiple_of(peer * rows, 8), rows)

    def one_copy(b, k):
        peer = dom_peer(k)
        return remote(
            part.at[b, slice_of(peer)],
            part_recv.at[b, k],
            one_send_sem.at[b, k],
            one_recv_sem.at[b, k],
            "dom",
            peer,
        )

    def two_copy(b, k):
        at = total.at[b, slice_of(d)]
        return remote(
            at, at, two_send_sem.at[b, k], two_recv_sem.at[b, k], "dom", dom_peer(k)
        )

    def from_peer(b, k):
        at = total.at[b, slice_of(dom_peer(doms - k))]
        return remote(
            at, at, two_send_sem.at[b, k], two_recv_sem.at[b, k], "dom", dom_peer(doms - k)
        )

    def all_reduce(b):
        def loop(body):
            def step(k, carry):
                body(k)
                return carry

            lax.fori_loop(1, doms, step, 0)

        loop(lambda k: one_copy(b, k).start())
        total[b, slice_of(d), :] = part[b, slice_of(d), :]

        def add(k):
            one_copy(b, k).wait_recv()
            total[b, slice_of(d), :] += part_recv[b, k]

        loop(add)
        loop(lambda k: two_copy(b, k).start())
        loop(lambda k: from_peer(b, k).wait_recv())

    def finish_reduce(b):
        def step(k, carry):
            one_copy(b, k).wait_send()
            two_copy(b, k).wait_send()
            return carry

        lax.fori_loop(1, doms, step, 0)

    def coefficients(b):
        gram = total[b, res : res + total_states, :]
        shape = (total_states, total_states)
        eye = (
            lax.broadcasted_iota(jnp.int32, shape, 0) == lax.broadcasted_iota(jnp.int32, shape, 1)
        ).astype(F32)
        along = jnp.sum(gram * eye, axis=0, keepdims=True) / total_nodes + EPSILON
        down = jnp.sum(gram * eye, axis=1, keepdims=True) / total_nodes + EPSILON
        root_i, root_j = lax.rsqrt(along), lax.rsqrt(down)
        mixing = root_i * (1.5 * eye - 0.5 * (gram * root_i * root_j / total_nodes))
        mix[b] = mixing.astype(BF16)
        for h in range(res // total_states):
            at = slice(h * total_states, (h + 1) * total_states)
            proj[b, :, at] = dot_nn(mixing, total[b, at, :], lax.Precision.HIGHEST).astype(BF16)

    def to(way):
        return s + 1 if way == RIGHT else s - 1

    origin = {RIGHT: s == 0, LEFT: s == sts - 1}
    sends = {RIGHT: has_right, LEFT: has_left}
    receives = {RIGHT: has_left, LEFT: has_right}
    near_end = {RIGHT: s == 1, LEFT: s == sts - 2}
    pieces = ((0, moved), (moved, cells))

    def near_copy(way, c):
        return remote(
            res_ref.at[c],
            res_near.at[way, c],
            near_send_sem.at[way, c],
            near_recv_sem.at[way, c],
            "st",
            to(way),
        )

    def near_start(c):
        for way in (RIGHT, LEFT):
            there = both(origin[way], sends[way])

            @pl.when(there)
            def _():
                near_copy(way, c).start()

            pending.append((there, partial(near_copy, way, c)))

    def near_wait():
        for way in (RIGHT, LEFT):

            @pl.when(near_end[way])
            def _():
                for c in range(moved):
                    near_copy(way, c).wait_recv()

    def coef_copy(b, way):
        return remote(
            proj.at[b],
            proj_near.at[way, b],
            coef_send_sem.at[way, b],
            coef_recv_sem.at[way, b],
            "st",
            to(way),
        )

    def coef_start(b):
        for way in (RIGHT, LEFT):
            there = both(origin[way], sends[way])

            @pl.when(there)
            def _():
                coef_copy(b, way).start()

            pending.append((there, partial(coef_copy, b, way)))

    def share_copy(b, t, way, piece):
        at = pl.ds(pieces[piece][0], pieces[piece][1] - pieces[piece][0])
        return remote(
            share.at[b, t, at],
            share_recv.at[way, b, t, at],
            share_send_sem.at[b, t, piece],
            share_recv_sem.at[way, b, t, piece],
            "st",
            to(way),
        )

    def targets():
        for j in range(sts - 1):
            far = sts - 1 - j
            yield far, RIGHT, far > s
            yield j, LEFT, j < s

    def share_start(b):
        def one(c, carry):
            found = dot_nt(proj[b], res_ref[c])
            for t in range(sts):
                share[b, t, c] = found[t * width : (t + 1) * width, :].astype(BF16)
            return carry

        lax.fori_loop(0, cells, one, 0)
        for t, way, ahead in targets():

            @pl.when(both(ahead, origin[way]))
            def _():
                share_copy(b, t, way, 1).start()

            for piece in (0, 1):
                there = ahead if piece else both(ahead, jnp.logical_not(origin[way]))
                pending.append((there, partial(share_copy, b, t, way, piece)))

    def retain(b):
        def one(c, carry):
            retained[b, c] = dot_nn(mix[b, own, :], states[b, c]) - dot_nt(
                proj[b, own, :], res_ref[c]
            )
            return carry

        lax.fori_loop(0, cells, one, 0)

    def near_share(b):
        for way in (RIGHT, LEFT):

            @pl.when(near_end[way])
            def _():
                coef_copy(b, way).wait_recv()
                for c in range(moved):
                    found = dot_nt(proj_near[way, b], res_near[way, c])
                    for t in range(sts):
                        passed = t > s if way == RIGHT else t < s

                        @pl.when(passed)
                        def _():
                            share[b, t, c] = (
                                share[b, t, c].astype(F32)
                                + found[t * width : (t + 1) * width, :]
                            ).astype(BF16)

                        @pl.when(t == s)
                        def _():
                            retained[b, c] -= found[t * width : (t + 1) * width, :]

    def share_forward(b, piece):
        for t, way, ahead in targets():

            @pl.when(both(ahead, jnp.logical_not(origin[way])))
            def _():
                def absorb():
                    share_copy(b, t, way, piece).wait_recv()

                    def one(c, carry):
                        share[b, t, c] = (
                            share[b, t, c].astype(F32) + share_recv[way, b, t, c].astype(F32)
                        ).astype(BF16)
                        return carry

                    lax.fori_loop(*pieces[piece], one, 0)

                if piece:
                    absorb()
                else:
                    pl.when(jnp.logical_not(near_end[way]))(absorb)
                share_copy(b, t, way, piece).start()

    def finish(b):
        for piece in (0, 1):
            for way in (RIGHT, LEFT):
                source = receives[way]
                if piece == 0:
                    source = both(source, jnp.logical_not(near_end[way]))

                @pl.when(source)
                def _():
                    share_copy(b, s, way, piece).wait_recv()

                    def one(c, carry):
                        retained[b, c] -= share_recv[way, b, s, c].astype(F32)
                        return carry

                    lax.fori_loop(*pieces[piece], one, 0)

            for c in range(*pieces[piece]):
                out_ref[b, c] = retained[b, c].astype(BF16) * mask(c)

    filter_block(0, first_chunks, last_chunks)
    for k in range(sts):
        gather_start(0, k)
    for c in range(moved):
        near_start(c)
    for b in range(1, blocks):
        filter_block(b)
    if blocks > 1:
        gather_start(1, 0)
    gather_steps(0)
    for b in range(blocks):
        contract(b)
        all_reduce(b)
        if b:
            share_forward(b - 1, 1)
        coefficients(b)
        coef_start(b)
        share_start(b)
        retain(b)
        if b + 1 < blocks:
            gather_steps(b + 1)
        if b == 0:
            near_wait()
        near_share(b)
        share_forward(b, 0)
        if b:
            finish(b - 1)
    share_forward(blocks - 1, 1)
    finish(blocks - 1)
    for there, make in pending:

        @pl.when(there)
        def _():
            make().wait_send()

    for b in range(blocks):
        finish_reduce(b)


def on_device(start_block, resident, stiffness, cell_scale, potential, cell_count, face_index):
    blocks, cells, width, nodes = start_block.shape
    res = resident.shape[0]
    face = face_index.shape[2]
    doms, sts = lax.axis_size("dom"), lax.axis_size("st")
    total_states = sts * width
    rows = -(-(res + total_states) // (8 * doms)) * 8
    moved = cells // 4
    sizes = (doms, sts, blocks, cells, width, nodes, face, res, rows, moved)
    dma = pltpu.SemaphoreType.DMA
    vmem = pl.BlockSpec(memory_space=pltpu.VMEM)
    smem = pl.BlockSpec(memory_space=pltpu.SMEM)
    return pl.pallas_call(
        partial(kernel, sizes),
        out_shape=jax.ShapeDtypeStruct((blocks, cells, width, nodes), BF16),
        in_specs=[smem, smem, vmem, pl.BlockSpec(memory_space=pl.ANY), vmem, vmem, vmem],
        out_specs=vmem,
        scratch_shapes=[
            pltpu.VMEM((cells * width, nodes), F32),
            pltpu.VMEM((cells * width, nodes), BF16),
            pltpu.VMEM((blocks, cells, total_states, nodes), BF16),
            pltpu.VMEM((blocks, doms * rows, total_states), F32),
            pltpu.VMEM((blocks, doms, rows, total_states), F32),
            pltpu.VMEM((blocks, doms * rows, total_states), F32),
            pltpu.VMEM((blocks, total_states, total_states), BF16),
            pltpu.VMEM((blocks, total_states, res), BF16),
            pltpu.VMEM((blocks, sts, cells, width, nodes), BF16),
            pltpu.VMEM((2, blocks, sts, cells, width, nodes), BF16),
            pltpu.VMEM((nodes, cells, res), BF16),
            pltpu.VMEM((res // 128, face * cells, 128), F32),
            pltpu.VMEM((cells, nodes, res), BF16),
            pltpu.VMEM((2, moved, nodes, res), BF16),
            pltpu.VMEM((2, blocks, total_states, res), BF16),
            pltpu.VMEM((blocks, cells, width, nodes), F32),
            pltpu.VMEM((2, blocks, 2, width, face), F32),
            pltpu.VMEM((2, blocks, 2, width, face), F32),
            dma((2, blocks, 2)),
            dma((2, blocks, 2)),
            dma((blocks, 2, sts)),
            dma((blocks, sts)),
            dma((blocks, doms)),
            dma((blocks, doms)),
            dma((blocks, doms)),
            dma((blocks, doms)),
            dma((blocks, sts, 2)),
            dma((2, blocks, sts, 2)),
            dma,
            dma((2, moved)),
            dma((2, moved)),
            dma((2, blocks)),
            dma((2, blocks)),
        ],
        compiler_params=pltpu.CompilerParams(
            collective_id=0, has_side_effects=True, vmem_limit_bytes=60 * 1024 * 1024
        ),
    )(
        cell_scale,
        cell_count,
        start_block,
        jnp.transpose(resident, (2, 1, 0)),
        stiffness,
        potential,
        face_index,
    )


def solution(mesh):
    return jax.shard_map(
        on_device,
        mesh=mesh,
        in_specs=(
            P(None, "dom", "st", None),
            P("st", "dom", None),
            P(),
            P("dom"),
            P("dom", None),
            P("dom"),
            P("dom", None, None),
        ),
        out_specs=P(None, "dom", "st", None),
        check_vma=False,
    )
```

```python
from functools import partial

import jax
import jax.numpy as jnp
from jax import lax
from jax.experimental import pallas as pl
from jax.experimental.pallas import tpu as pltpu
from jax.sharding import PartitionSpec as P

CENTER = 0.5
HALF_WIDTH = 2.0
EPSILON = 1e-06
F32 = jnp.float32
BF16 = jnp.bfloat16
RIGHT, LEFT = 0, 1


def dot_nn(a, b, precision=None):
    return lax.dot_general(
        a, b, (((1,), (0,)), ((), ())), precision=precision, preferred_element_type=F32
    )


def dot_nt(a, b, precision=None):
    return lax.dot_general(
        a, b, (((1,), (1,)), ((), ())), precision=precision, preferred_element_type=F32
    )


def kernel(
    sizes,
    scale_ref,
    count_ref,
    start_ref,
    res_hbm,
    stiff_ref,
    pot_ref,
    face_ref,
    out_ref,
    local,
    inner,
    states,
    part,
    part_recv,
    total,
    mix,
    proj,
    share,
    share_recv,
    res_in,
    res_wide,
    res_ref,
    res_near,
    proj_near,
    retained,
    face_out,
    face_in,
    face_send_sem,
    face_recv_sem,
    gather_send_sem,
    gather_recv_sem,
    one_send_sem,
    one_recv_sem,
    two_send_sem,
    two_recv_sem,
    share_send_sem,
    share_recv_sem,
    load_sem,
    near_send_sem,
    near_recv_sem,
    coef_send_sem,
    coef_recv_sem,
):
    doms, sts, blocks, cells, width, nodes, face, res, rows, moved = sizes
    total_states = sts * width
    total_nodes = float(doms * cells * nodes)
    window = (nodes - face) // 128 * 128
    offset = nodes - face - window
    d = lax.axis_index("dom")
    s = lax.axis_index("st")
    has_right, has_left = s < sts - 1, s > 0
    has_next, has_prev = d < doms - 1, d > 0
    own = pl.ds(pl.multiple_of(s * width, width), width)
    pending = []
    both = jnp.logical_and
    count = count_ref[0]
    scale = [scale_ref[c] for c in range(cells)]
    live = [jnp.where(c < count, 1.0, 0.0).astype(F32) for c in range(cells)]
    last = [jnp.where(c == count - 1, 1.0, 0.0).astype(F32) for c in range(cells)]
    load = pltpu.make_async_copy(res_hbm, res_in, load_sem)
    load.start()

    def dom_peer(k):
        return lax.rem(d + k, doms)

    barrier = pltpu.get_barrier_semaphore()

    def greet(k, carry):
        pl.semaphore_signal(
            barrier, inc=1, device_id={"dom": dom_peer(k)}, device_id_type=pl.DeviceIdType.MESH
        )
        return carry

    lax.fori_loop(1, doms, greet, 0)

    @pl.when(has_right)
    def _():
        pl.semaphore_signal(
            barrier, inc=1, device_id={"st": s + 1}, device_id_type=pl.DeviceIdType.MESH
        )

    @pl.when(has_left)
    def _():
        pl.semaphore_signal(
            barrier, inc=1, device_id={"st": s - 1}, device_id_type=pl.DeviceIdType.MESH
        )

    neighbours = has_right.astype(jnp.int32) + has_left.astype(jnp.int32)
    pl.semaphore_wait(barrier, doms - 1 + neighbours)

    def remote(src, dst, send_sem, recv_sem, axis, peer):
        return pltpu.make_async_remote_copy(
            src_ref=src,
            dst_ref=dst,
            send_sem=send_sem,
            recv_sem=recv_sem,
            device_id={axis: peer},
            device_id_type=pl.DeviceIdType.MESH,
        )

    def one_hot(row, first, extent):
        node = lax.broadcasted_iota(jnp.int32, (extent, face), 0) + first
        if row == 0:
            node = node + (count - 1) * nodes
        return jnp.where(face_ref[0, row : row + 1, :] == node, 1.0, 0.0).astype(F32)

    def mask(c):
        return live[c].astype(BF16)

    def relayout(chunk):
        at = slice(chunk * face, (chunk + 1) * face)
        wide = res_in[at].astype(F32).reshape(face * cells, res)
        for h in range(res // 128):
            lanes = slice(h * 128, (h + 1) * 128)
            res_wide[h] = wide[:, lanes]
            for c in range(cells):
                res_ref[c, at, lanes] = res_wide[h, pl.ds(c, face, stride=cells), :].astype(BF16)

    chunks = nodes // face

    def first_chunks():
        load.wait()
        for chunk in range(chunks // 2):
            relayout(chunk)

    def last_chunks():
        for chunk in range(chunks // 2, chunks):
            relayout(chunk)

    def rows_of(c):
        return slice(c * width, (c + 1) * width)

    def face_copy(step, b, way):
        return remote(
            face_out.at[step, b, way],
            face_in.at[step, b, way],
            face_send_sem.at[step, b, way],
            face_recv_sem.at[step, b, way],
            "dom",
            d + 1 if way == RIGHT else d - 1,
        )

    def apply_operator(step, b, field, meanwhile=None):
        local[...] = dot_nn(field(None), stiff_ref[...])
        last_tail = jnp.zeros((width, nodes - window), F32)
        for c in range(cells):
            value = scale[c] * local[rows_of(c), :] + pot_ref[c : c + 1, :] * field(
                c
            ).astype(F32)
            local[rows_of(c), :] = value
            last_tail = last_tail + last[c] * value[:, window:]
        face_out[step, b, RIGHT] = dot_nn(
            last_tail, one_hot(0, window, nodes - window), lax.Precision.HIGHEST
        )
        face_out[step, b, LEFT] = dot_nn(
            local[rows_of(0), :face], one_hot(1, 0, face), lax.Precision.HIGHEST
        )
        for way, there in ((RIGHT, has_next), (LEFT, has_prev)):

            @pl.when(there)
            def _():
                face_copy(step, b, way).start()

            pending.append((there, partial(face_copy, step, b, way)))
        for c in range(cells - 1):
            pair = live[c + 1]
            tail = local[rows_of(c), window:]
            head = local[rows_of(c + 1), :face]
            padded = head
            if offset:
                padded = jnp.concatenate([jnp.zeros((width, offset), F32), head], axis=1)
            local[rows_of(c), window:] = tail + pair * padded
            local[rows_of(c + 1), :face] = head + pair * tail[:, offset:]
        if meanwhile is not None:
            meanwhile()
        for way, source in ((RIGHT, has_prev), (LEFT, has_next)):

            @pl.when(source)
            def _():
                face_copy(step, b, way).wait_recv()

            @pl.when(jnp.logical_not(source))
            def _():
                face_in[step, b, way] = jnp.zeros((width, face), F32)

        local[rows_of(0), :face] += dot_nt(
            face_in[step, b, RIGHT], one_hot(1, 0, face), lax.Precision.HIGHEST
        )
        tail_add = dot_nt(
            face_in[step, b, LEFT], one_hot(0, window, nodes - window), lax.Precision.HIGHEST
        )
        for c in range(cells):
            local[rows_of(c), window:] += last[c] * tail_add

    def filter_block(b, one=None, two=None):
        def first(c):
            if c is None:
                parts = [first(i) for i in range(cells)]
                return jnp.concatenate(parts, axis=0)
            return start_ref[b, c] * mask(c)

        def second(c):
            return inner[...] if c is None else inner[rows_of(c), :]

        apply_operator(0, b, first, one)
        for c in range(cells):
            value = live[c] * local[rows_of(c), :]
            inner[rows_of(c), :] = ((value - CENTER * first(c).astype(F32)) / HALF_WIDTH).astype(
                BF16
            )
        apply_operator(1, b, second, two)
        for c in range(cells):
            value = live[c] * local[rows_of(c), :]
            states[b, c, own, :] = (
                2.0 * (value - CENTER * second(c).astype(F32)) / HALF_WIDTH - first(c).astype(F32)
            ).astype(BF16)

    def gather_copy(b, way, shard):
        at = states.at[b, :, pl.ds(pl.multiple_of(shard * width, width), width), :]
        return remote(
            at,
            at,
            gather_send_sem.at[b, way, shard],
            gather_recv_sem.at[b, shard],
            "st",
            s + 1 if way == RIGHT else s - 1,
        )

    def gather_send(b, way, shard, there):
        @pl.when(there)
        def _():
            gather_copy(b, way, shard).start()

        pending.append((there, partial(gather_copy, b, way, shard)))

    def gather_start(b, k):
        gather_send(b, RIGHT, s, both(has_right, s == k))
        gather_send(b, LEFT, s, both(has_left, s + k == sts - 1))

    def gather_steps(b):
        for k in range(1, sts):
            for way, shard, here, more in (
                (RIGHT, s - k, s >= k, has_right),
                (LEFT, s + k, s + k < sts, has_left),
            ):

                @pl.when(here)
                def _():
                    gather_copy(b, way, shard).wait_recv()

                gather_send(b, way, shard, both(here, more))
            if b + 1 < blocks:
                gather_start(b + 1, k)

    def contract(b):
        part[b] = jnp.zeros(part.shape[1:], F32)

        def add_cell(c, carry):
            block = states[b, c]
            found = dot_nn(block, res_ref[c])
            for h in range(res // total_states):
                at = slice(h * total_states, (h + 1) * total_states)
                part[b, at, :] += found[:, at]
            part[b, res : res + total_states, :] += dot_nt(block, block)
            return carry

        lax.fori_loop(0, cells, add_cell, 0)

    def slice_of(peer):
        return pl.ds(pl.multiple_of(peer * rows, 8), rows)

    def one_copy(b, k):
        peer = dom_peer(k)
        return remote(
            part.at[b, slice_of(peer)],
            part_recv.at[b, k],
            one_send_sem.at[b, k],
            one_recv_sem.at[b, k],
            "dom",
            peer,
        )

    def two_copy(b, k):
        at = total.at[b, slice_of(d)]
        return remote(
            at, at, two_send_sem.at[b, k], two_recv_sem.at[b, k], "dom", dom_peer(k)
        )

    def from_peer(b, k):
        at = total.at[b, slice_of(dom_peer(doms - k))]
        return remote(
            at, at, two_send_sem.at[b, k], two_recv_sem.at[b, k], "dom", dom_peer(doms - k)
        )

    def all_reduce(b):
        def loop(body):
            def step(k, carry):
                body(k)
                return carry

            lax.fori_loop(1, doms, step, 0)

        loop(lambda k: one_copy(b, k).start())
        total[b, slice_of(d), :] = part[b, slice_of(d), :]

        def add(k):
            one_copy(b, k).wait_recv()
            total[b, slice_of(d), :] += part_recv[b, k]

        loop(add)
        loop(lambda k: two_copy(b, k).start())
        loop(lambda k: from_peer(b, k).wait_recv())

    def finish_reduce(b):
        def step(k, carry):
            one_copy(b, k).wait_send()
            two_copy(b, k).wait_send()
            return carry

        lax.fori_loop(1, doms, step, 0)

    def coefficients(b):
        gram = total[b, res : res + total_states, :]
        shape = (total_states, total_states)
        eye = (
            lax.broadcasted_iota(jnp.int32, shape, 0) == lax.broadcasted_iota(jnp.int32, shape, 1)
        ).astype(F32)
        along = jnp.sum(gram * eye, axis=0, keepdims=True) / total_nodes + EPSILON
        down = jnp.sum(gram * eye, axis=1, keepdims=True) / total_nodes + EPSILON
        root_i, root_j = lax.rsqrt(along), lax.rsqrt(down)
        mixing = root_i * (1.5 * eye - 0.5 * (gram * root_i * root_j / total_nodes))
        mix[b] = mixing.astype(BF16)
        for h in range(res // total_states):
            at = slice(h * total_states, (h + 1) * total_states)
            proj[b, :, at] = dot_nn(mixing, total[b, at, :], lax.Precision.HIGHEST).astype(BF16)

    def to(way):
        return s + 1 if way == RIGHT else s - 1

    origin = {RIGHT: s == 0, LEFT: s == sts - 1}
    sends = {RIGHT: has_right, LEFT: has_left}
    receives = {RIGHT: has_left, LEFT: has_right}
    near_end = {RIGHT: s == 1, LEFT: s == sts - 2}
    pieces = ((0, moved), (moved, cells))

    def near_copy(way, c):
        return remote(
            res_ref.at[c],
            res_near.at[way, c],
            near_send_sem.at[way, c],
            near_recv_sem.at[way, c],
            "st",
            to(way),
        )

    def near_start(c):
        for way in (RIGHT, LEFT):
            there = both(origin[way], sends[way])

            @pl.when(there)
            def _():
                near_copy(way, c).start()

            pending.append((there, partial(near_copy, way, c)))

    def near_wait():
        for way in (RIGHT, LEFT):

            @pl.when(near_end[way])
            def _():
                for c in range(moved):
                    near_copy(way, c).wait_recv()

    def coef_copy(b, way):
        return remote(
            proj.at[b],
            proj_near.at[way, b],
            coef_send_sem.at[way, b],
            coef_recv_sem.at[way, b],
            "st",
            to(way),
        )

    def coef_start(b):
        for way in (RIGHT, LEFT):
            there = both(origin[way], sends[way])

            @pl.when(there)
            def _():
                coef_copy(b, way).start()

            pending.append((there, partial(coef_copy, b, way)))

    def share_copy(b, t, way, piece):
        at = pl.ds(pieces[piece][0], pieces[piece][1] - pieces[piece][0])
        return remote(
            share.at[b, t, at],
            share_recv.at[way, b, t, at],
            share_send_sem.at[b, t, piece],
            share_recv_sem.at[way, b, t, piece],
            "st",
            to(way),
        )

    def targets():
        for j in range(sts - 1):
            far = sts - 1 - j
            yield far, RIGHT, far > s
            yield j, LEFT, j < s

    def share_start(b):
        def one(c, carry):
            found = dot_nt(proj[b], res_ref[c])
            for t in range(sts):
                share[b, t, c] = found[t * width : (t + 1) * width, :].astype(BF16)

                @pl.when(t == s)
                def _():
                    retained[b, c] = -found[t * width : (t + 1) * width, :]

            return carry

        lax.fori_loop(0, cells, one, 0)
        for t, way, ahead in targets():

            @pl.when(both(ahead, origin[way]))
            def _():
                share_copy(b, t, way, 1).start()

            for piece in (0, 1):
                there = ahead if piece else both(ahead, jnp.logical_not(origin[way]))
                pending.append((there, partial(share_copy, b, t, way, piece)))

    def retain(b):
        def one(c, carry):
            retained[b, c] += dot_nn(mix[b, own, :], states[b, c])
            return carry

        lax.fori_loop(0, cells, one, 0)

    def near_share(b):
        for way in (RIGHT, LEFT):

            @pl.when(near_end[way])
            def _():
                coef_copy(b, way).wait_recv()
                for c in range(moved):
                    found = dot_nt(proj_near[way, b], res_near[way, c])
                    for t in range(sts):
                        passed = t > s if way == RIGHT else t < s

                        @pl.when(passed)
                        def _():
                            share[b, t, c] = (
                                share[b, t, c].astype(F32)
                                + found[t * width : (t + 1) * width, :]
                            ).astype(BF16)

                        @pl.when(t == s)
                        def _():
                            retained[b, c] -= found[t * width : (t + 1) * width, :]

    def share_forward(b, piece):
        for t, way, ahead in targets():

            @pl.when(both(ahead, jnp.logical_not(origin[way])))
            def _():
                def absorb():
                    share_copy(b, t, way, piece).wait_recv()

                    def one(c, carry):
                        share[b, t, c] = (
                            share[b, t, c].astype(F32) + share_recv[way, b, t, c].astype(F32)
                        ).astype(BF16)
                        return carry

                    lax.fori_loop(*pieces[piece], one, 0)

                if piece:
                    absorb()
                else:
                    pl.when(jnp.logical_not(near_end[way]))(absorb)
                share_copy(b, t, way, piece).start()

    def finish(b):
        for piece in (0, 1):
            for way in (RIGHT, LEFT):
                source = receives[way]
                if piece == 0:
                    source = both(source, jnp.logical_not(near_end[way]))

                @pl.when(source)
                def _():
                    share_copy(b, s, way, piece).wait_recv()

                    def one(c, carry):
                        retained[b, c] -= share_recv[way, b, s, c].astype(F32)
                        return carry

                    lax.fori_loop(*pieces[piece], one, 0)

            for c in range(*pieces[piece]):
                out_ref[b, c] = retained[b, c].astype(BF16) * mask(c)

    filter_block(0, first_chunks, last_chunks)
    for k in range(sts):
        gather_start(0, k)
    near_start(0)
    for b in range(1, blocks):
        filter_block(b)
    if blocks > 1:
        gather_start(1, 0)
    for c in range(1, moved):
        near_start(c)
    gather_steps(0)
    for b in range(blocks):
        contract(b)
        all_reduce(b)
        if b:
            share_forward(b - 1, 1)
        coefficients(b)
        coef_start(b)
        share_start(b)
        if b + 1 < blocks:
            gather_steps(b + 1)
        if b == 0:
            near_wait()
        near_share(b)
        share_forward(b, 0)
        retain(b)
        if b:
            finish(b - 1)
    share_forward(blocks - 1, 1)
    finish(blocks - 1)
    for there, make in pending:

        @pl.when(there)
        def _():
            make().wait_send()

    for b in range(blocks):
        finish_reduce(b)


def on_device(start_block, resident, stiffness, cell_scale, potential, cell_count, face_index):
    blocks, cells, width, nodes = start_block.shape
    res = resident.shape[0]
    face = face_index.shape[2]
    doms, sts = lax.axis_size("dom"), lax.axis_size("st")
    total_states = sts * width
    rows = -(-(res + total_states) // (8 * doms)) * 8
    moved = 3 * cells // 8
    sizes = (doms, sts, blocks, cells, width, nodes, face, res, rows, moved)
    dma = pltpu.SemaphoreType.DMA
    vmem = pl.BlockSpec(memory_space=pltpu.VMEM)
    smem = pl.BlockSpec(memory_space=pltpu.SMEM)
    return pl.pallas_call(
        partial(kernel, sizes),
        out_shape=jax.ShapeDtypeStruct((blocks, cells, width, nodes), BF16),
        in_specs=[smem, smem, vmem, pl.BlockSpec(memory_space=pl.ANY), vmem, vmem, vmem],
        out_specs=vmem,
        scratch_shapes=[
            pltpu.VMEM((cells * width, nodes), F32),
            pltpu.VMEM((cells * width, nodes), BF16),
            pltpu.VMEM((blocks, cells, total_states, nodes), BF16),
            pltpu.VMEM((blocks, doms * rows, total_states), F32),
            pltpu.VMEM((blocks, doms, rows, total_states), F32),
            pltpu.VMEM((blocks, doms * rows, total_states), F32),
            pltpu.VMEM((blocks, total_states, total_states), BF16),
            pltpu.VMEM((blocks, total_states, res), BF16),
            pltpu.VMEM((blocks, sts, cells, width, nodes), BF16),
            pltpu.VMEM((2, blocks, sts, cells, width, nodes), BF16),
            pltpu.VMEM((nodes, cells, res), BF16),
            pltpu.VMEM((res // 128, face * cells, 128), F32),
            pltpu.VMEM((cells, nodes, res), BF16),
            pltpu.VMEM((2, moved, nodes, res), BF16),
            pltpu.VMEM((2, blocks, total_states, res), BF16),
            pltpu.VMEM((blocks, cells, width, nodes), F32),
            pltpu.VMEM((2, blocks, 2, width, face), F32),
            pltpu.VMEM((2, blocks, 2, width, face), F32),
            dma((2, blocks, 2)),
            dma((2, blocks, 2)),
            dma((blocks, 2, sts)),
            dma((blocks, sts)),
            dma((blocks, doms)),
            dma((blocks, doms)),
            dma((blocks, doms)),
            dma((blocks, doms)),
            dma((blocks, sts, 2)),
            dma((2, blocks, sts, 2)),
            dma,
            dma((2, moved)),
            dma((2, moved)),
            dma((2, blocks)),
            dma((2, blocks)),
        ],
        compiler_params=pltpu.CompilerParams(
            collective_id=0, has_side_effects=True, vmem_limit_bytes=60 * 1024 * 1024
        ),
    )(
        cell_scale,
        cell_count,
        start_block,
        jnp.transpose(resident, (2, 1, 0)),
        stiffness,
        potential,
        face_index,
    )


def solution(mesh):
    return jax.shard_map(
        on_device,
        mesh=mesh,
        in_specs=(
            P(None, "dom", "st", None),
            P("st", "dom", None),
            P(),
            P("dom"),
            P("dom", None),
            P("dom"),
            P("dom", None, None),
        ),
        out_specs=P(None, "dom", "st", None),
        check_vma=False,
    )
```
